32 devices in a mesh: dom: 8 (over z, x), sub: 4 (over y, core).
Axes of the slice: x: 2, y: 2, z: 4, core: 2. Of those that a mesh axis runs over, the one named last changes fastest.
Arguments:
- rhs: float32 [8192, 832], P(('dom', 'sub')), may hold values from -6 to 6
- elem_block: bfloat16 [8192, 64, 64], P(('dom', 'sub')), may hold values from -0.5 to 2.5
- block_inv: bfloat16 [8192, 64, 64], P(('dom', 'sub')), may hold values from -0.2 to 0.8
- flux_jac: float32 [13, 13], replicated, may hold values from -1.75 to 1.75
- face_src: int32 [8192, 6], P(('dom', 'sub')), may hold values from 0 to 2175
- send_face: int32 [160, 128], P(('dom', 'sub')), may hold values from 0 to 1535
- elem_route: int32 [8192], P(('dom', 'sub')), may hold values from 0 to 63
- agg_local: int32 [1024, 2], P(('dom', 'sub')), may hold values from 0 to 63
- coarse_block: float32 [2048, 4, 4], P(('dom', 'sub')), may hold values from -0.5 to 1.3
- coarse_inv: float32 [2048, 4, 4], P(('dom', 'sub')), may hold values from -1 to 4
Outputs:
- adjoint: float32 [8192, 832], P(('dom', 'sub'))
The draws below stay inside these ranges and needn't reach their ends.
Inputs may be any that keep to these rules, and one draw needn't show every extreme that they name: `elem_route`: any owner may receive any slot from any device.
All inputs are finite; a program needn't handle non-finite values.
Results may differ from the reference program's by a relative error of at most 0.0081.
Values sent between devices are 32-bit elements; how exact they have to be, the bound alone decides.
A program may use at most 128 MiB of HBM per device.

```python
import math
import jax
import jax.numpy as jnp
import numpy as np
from jax import lax

COMPS = 13
NODES = 64
FACES = 6
FACE_NODES = 16
MODES = 4
ROUNDS = 5
MOST = 2
ELEM_DEV = 256
SLOTS = 128
AGG_DEV = 64
ELEMS = 8192
AGGS = 2048
DEVICES = 32


def blocked(key, count, width, diag_lo, diag_hi, spread, bound):
    key_diag = jax.random.fold_in(key, 11)
    key_off = jax.random.fold_in(key, 12)
    diagonal = jax.random.uniform(key_diag, (count, width), jnp.float32, diag_lo, diag_hi)
    off = jax.random.normal(key_off, (count, width, width), jnp.float32) * spread
    off = jnp.clip(off, -bound, bound)
    eye = jnp.eye(width, dtype=jnp.float32)
    return off * (1.0 - eye) + eye * diagonal[:, :, None]


def draw_elem_block(key, part):
    return blocked(key, ELEMS, NODES, 1.0, 2.0, 0.1, 0.5).astype(jnp.bfloat16)


def draw_block_inv(key, part):
    return blocked(key, ELEMS, NODES, 0.3, 0.6, 0.04, 0.19).astype(jnp.bfloat16)


def draw_coarse_block(key, part):
    return blocked(key, AGGS, MODES, 0.4, 0.8, 0.1, 0.5)


def draw_coarse_inv(key, part):
    return blocked(key, AGGS, MODES, 1.5, 3.0, 0.2, 1.0)


def set_ends(entries, own_key, low, top_value):
    shape = entries.shape
    place = [jax.random.randint(jax.random.fold_in(own_key, axis), (), 0, shape[axis]) for axis in range(len(shape))]
    entries = entries.at[tuple(place)].set(low)
    longest = shape.index(max(shape))
    place[longest] = (place[longest] + 1) % shape[longest]
    return entries.at[tuple(place)].set(top_value)


def levels(own_key, extent, shards, least, top_value):
    def one(dim, blocks):
        steps = jax.random.uniform(jax.random.fold_in(jax.random.fold_in(own_key, 6), dim), (blocks,), jnp.float32, least / len(shards), top_value / len(shards))
        return jnp.repeat(jnp.exp(steps), extent[dim] // blocks).reshape((-1,) + (1,) * (len(extent) - dim - 1))

    gain = one(*shards[0])
    for cut in shards[1:]:
        gain = gain * one(*cut)
    return gain


def scatter_about(own_key, dims, deviation, most, cuts=(), held_as=jnp.bfloat16):
    values = jax.random.normal(own_key, dims, jnp.float32) * deviation
    if len(cuts) > 0:
        values = levels(own_key, dims, cuts, -0.22, 0.18) * values
    return jnp.clip(values, min=-most, max=most).astype(held_as)


def setup_inputs(seed: int = 0) -> dict:
    streams_of = jax.random.split(jax.random.key(seed), 11)
    rhs = scatter_about(streams_of[0], (ELEMS, COMPS * NODES), 1.0, 6.0, ((0, 32),), jnp.float32)
    elem_block = draw_elem_block(jax.random.fold_in(streams_of[10], 71), 0)
    block_inv = draw_block_inv(jax.random.fold_in(streams_of[10], 71), 0)
    flux_jac = scatter_about(streams_of[3], (COMPS, COMPS), COMPS ** -0.5, 1.75, (), jnp.float32)
    face_src = set_ends(jax.random.randint(streams_of[4], (ELEMS, FACES), 0, FACES * ELEM_DEV + ROUNDS * SLOTS), jax.random.fold_in(streams_of[4], 1), 0, (FACES * ELEM_DEV + ROUNDS * SLOTS) - 1).astype(jnp.int32)
    send_face = set_ends(jax.random.randint(streams_of[5], (DEVICES * ROUNDS, SLOTS), 0, FACES * ELEM_DEV), jax.random.fold_in(streams_of[5], 1), 0, (FACES * ELEM_DEV) - 1).astype(jnp.int32)
    elem_route = set_ends(jax.random.randint(streams_of[6], (ELEMS,), 0, DEVICES * MOST), jax.random.fold_in(streams_of[6], 1), 0, (DEVICES * MOST) - 1).astype(jnp.int32)
    agg_local = set_ends(jax.random.randint(streams_of[7], (DEVICES * DEVICES, MOST), 0, AGG_DEV), jax.random.fold_in(streams_of[7], 1), 0, AGG_DEV - 1).astype(jnp.int32)
    coarse_block = draw_coarse_block(jax.random.fold_in(streams_of[10], 71), 0)
    coarse_inv = draw_coarse_inv(jax.random.fold_in(streams_of[10], 71), 0)
    return {"rhs": rhs, "elem_block": elem_block, "block_inv": block_inv, "flux_jac": flux_jac, "face_src": face_src, "send_face": send_face, "elem_route": elem_route, "agg_local": agg_local, "coarse_block": coarse_block, "coarse_inv": coarse_inv}


HIGHEST = lax.Precision.HIGHEST
PENALTY = 0.5

def node_tables():
    points = np.array([-1.0, -1.0 / math.sqrt(5.0), 1.0 / math.sqrt(5.0), 1.0])
    weights = np.array([1.0, 5.0, 5.0, 1.0]) / 6.0
    grid_i, grid_j, grid_k = np.meshgrid(points, points, points, indexing='ij')
    weight_grid = weights[:, None, None] * weights[None, :, None] * weights[None, None, :] / 8.0
    basis = np.stack([np.ones(64), grid_i.reshape(-1), grid_j.reshape(-1), grid_k.reshape(-1)])
    restrict = basis * weight_grid.reshape(-1)[None, :]
    number = np.arange(64).reshape(4, 4, 4)
    sides = [number[0], number[3], number[:, 0], number[:, 3], number[:, :, 0], number[:, :, 3]]
    face_index = np.stack([side.reshape(-1) for side in sides])
    lift = np.eye(64)[face_index]
    return (basis, restrict, face_index, lift)

def block_apply(pair):
    blocks, field = pair
    rounded = field.astype(jnp.bfloat16).astype(jnp.float32)
    return jnp.einsum('enk,eck->ecn', blocks.astype(jnp.float32), rounded, precision=HIGHEST)

def operate(field, blocks_r, flux_jac, face_rows, send_r, face_index, lift):
    volume = lax.map(block_apply, (blocks_r, field))
    trace = field[:, :, :, face_index.reshape(-1)]
    trace = trace.reshape(DEVICES, ELEM_DEV, COMPS, FACES, FACE_NODES)
    trace = trace.transpose(0, 1, 3, 2, 4).reshape(DEVICES, ELEM_DEV * FACES, COMPS * FACE_NODES)
    received = []
    for round_no in range(ROUNDS):
        partner = jnp.bitwise_xor(jnp.arange(DEVICES, dtype=jnp.int32), jnp.int32(1 << round_no))
        picked = send_r[partner, round_no]
        received.append(trace[partner[:, None], picked])
    table = jnp.concatenate([trace] + received, axis=1)
    beside = jnp.take_along_axis(table, face_rows[:, :, None], axis=1)
    jump = (trace - beside).reshape(DEVICES, ELEM_DEV, FACES, COMPS, FACE_NODES)
    flux = PENALTY * jnp.einsum('defaq,ac->defcq', jump, flux_jac, precision=HIGHEST)
    lifted = jnp.einsum('defcq,fqn->decn', flux, jnp.asarray(lift, jnp.float32), precision=HIGHEST)
    return volume + lifted

def coarse_solve(coarse_rhs, blocks, inverse):
    first = jnp.einsum('amk,ack->acm', inverse, coarse_rhs, precision=HIGHEST)
    left = coarse_rhs - jnp.einsum('amk,ack->acm', blocks, first, precision=HIGHEST)
    return first + jnp.einsum('amk,ack->acm', inverse, left, precision=HIGHEST)

def reference(rhs, elem_block, block_inv, flux_jac, face_src, send_face, elem_route, agg_local, coarse_block, coarse_inv):
    basis, restrict, face_index, lift = node_tables()
    blocks_r = elem_block.reshape(DEVICES, ELEM_DEV, NODES, NODES)
    inverse_r = block_inv.reshape(DEVICES, ELEM_DEV, NODES, NODES)
    source = rhs.reshape(DEVICES, ELEM_DEV, COMPS, NODES)
    face_rows = face_src.reshape(DEVICES, ELEM_DEV * FACES)
    send_r = send_face.reshape(DEVICES, ROUNDS, SLOTS)

    def apply_op(field):
        return operate(field, blocks_r, flux_jac, face_rows, send_r, face_index, lift)

    def sweep(state):
        return state + lax.map(block_apply, (inverse_r, source - apply_op(state)))
    first = lax.map(block_apply, (inverse_r, source))
    second = sweep(first)
    resid = source - apply_op(second)
    partial_value = jnp.einsum('decn,mn->decm', resid, jnp.asarray(restrict, jnp.float32), precision=HIGHEST)
    partial_value = partial_value.reshape(ELEMS, COMPS * MODES)
    owner = elem_route // MOST
    slot = elem_route % MOST
    home = jnp.arange(ELEMS, dtype=jnp.int32) // ELEM_DEV
    agg_r = agg_local.reshape(DEVICES, DEVICES, MOST)
    global_id = (owner * AGG_DEV + agg_r[owner, home, slot]).astype(jnp.int32)
    coarse_rhs = jax.ops.segment_sum(partial_value, global_id, AGGS).reshape(AGGS, COMPS, MODES)
    coarse = coarse_solve(coarse_rhs, coarse_block, coarse_inv).reshape(AGGS, COMPS * MODES)
    correction = coarse[global_id].reshape(DEVICES, ELEM_DEV, COMPS, MODES)
    third = second + jnp.einsum('decm,mn->decn', correction, jnp.asarray(basis, jnp.float32), precision=HIGHEST)
    fourth = sweep(third)
    fifth = sweep(fourth)
    return fifth.reshape(ELEMS, COMPS * NODES)
```

```python
import functools
import math

import jax
import jax.numpy as jnp
import numpy as np
from jax import lax
from jax.experimental import pallas as pl
from jax.experimental.pallas import tpu as pltpu
from jax.sharding import PartitionSpec as P

COMPS = 13
NODES = 64
FACES = 6
FACE_NODES = 16
MODES = 4
ROUNDS = 5
MOST = 2
FLAT = COMPS * NODES
SIDE = COMPS * FACE_NODES
TRACE = FACES * SIDE

HIGHEST = lax.Precision.HIGHEST
PENALTY = 0.5
MESH = pl.DeviceIdType.MESH


def node_tables():
    points = np.array([-1.0, -1.0 / math.sqrt(5.0), 1.0 / math.sqrt(5.0), 1.0])
    weights = np.array([1.0, 5.0, 5.0, 1.0]) / 6.0
    grid_i, grid_j, grid_k = np.meshgrid(points, points, points, indexing="ij")
    weight_grid = weights[:, None, None] * weights[None, :, None] * weights[None, None, :] / 8.0
    basis = np.stack([np.ones(64), grid_i.reshape(-1), grid_j.reshape(-1), grid_k.reshape(-1)])
    restrict = basis * weight_grid.reshape(-1)[None, :]
    number = np.arange(64).reshape(4, 4, 4)
    sides = [number[0], number[3], number[:, 0], number[:, 3], number[:, :, 0], number[:, :, 3]]
    face_index = np.stack([side.reshape(-1) for side in sides])
    return basis, restrict, face_index


def const_tables():
    basis, restrict, face_index = node_tables()
    eye = np.eye(COMPS)
    row_comp = np.tile(np.repeat(eye, FACE_NODES, axis=0), (FACES, 1))
    row_comp = np.pad(row_comp, ((0, 0), (0, 3)))
    col_comp = np.pad(np.repeat(eye, NODES, axis=0), ((0, 0), (0, 3)))
    node = np.eye(NODES)[face_index]
    row_node = np.broadcast_to(node[:, None], (FACES, COMPS, FACE_NODES, NODES)).reshape(TRACE, NODES)
    col_node = np.tile(np.eye(NODES), (COMPS, 1))
    restrict_t = np.zeros((128, FLAT))
    restrict_t[: COMPS * MODES] = np.kron(eye, restrict)
    basis_t = np.zeros((FLAT, 128))
    basis_t[:, : COMPS * MODES] = np.kron(eye, basis.T)
    pick = np.zeros((128, MODES * 128))
    coef = np.zeros((16, MODES * 128))
    for k in range(MODES):
        for c in range(COMPS):
            for m in range(MODES):
                pick[c * MODES + k, k * 128 + c * MODES + m] = 1.0
                coef[m * MODES + k, k * 128 + c * MODES + m] = 1.0
    half = jnp.bfloat16
    return (
        jnp.asarray(row_comp, half),
        jnp.asarray(row_node, half),
        jnp.asarray(col_comp.T, half),
        jnp.asarray(col_node.T, half),
        jnp.asarray(col_comp, half),
        jnp.asarray(col_node, half),
        jnp.asarray(row_comp.T, half),
        jnp.asarray(row_node.T, half),
        jnp.asarray(restrict_t, jnp.float32),
        jnp.asarray(basis_t, jnp.float32),
        jnp.asarray(pick, jnp.float32),
        jnp.asarray(coef, jnp.float32),
    )


def dot(a, b):
    return jnp.dot(a, b, preferred_element_type=jnp.float32)


def dot_exact(a, b, dims=((1,), (0,))):
    return lax.dot_general(
        a, b, (dims, ((), ())), precision=HIGHEST, preferred_element_type=jnp.float32
    )


def kernel(
    count, subs,
    rhs, blocks, inverse, jac, face_src, send_face, route, agg_col, agg_row, cblock, cinv,
    row_comp, row_node, comp_col, node_col, col_comp, col_node, comp_row, node_row,
    restrict_t, basis_t, pick, coef,
    out,
    block_t, inverse_t, bcast, lift_t, trace_t, pick_local, pick_remote, pick_send,
    half_field, state, work, lifted, trace, beside, table, jump, sending, arriving,
    bucket, incoming, reply, answer,
    send_sem, recv_sem, give_sem, take_sem, back_sem, home_sem,
):
    elements = rhs.shape[1]
    tiles = elements // 128
    own = FACES * elements
    far = ROUNDS * 128
    me = lax.axis_index("dom") * subs + lax.axis_index("sub")

    def place(flat):
        return (flat // subs, flat % subs)

    def partner(k):
        bit = 1 << k
        return me + bit * (1 - 2 * ((me // bit) % 2))

    barrier = pltpu.get_barrier_semaphore()

    def greet(step, carry):
        pl.semaphore_signal(
            barrier, inc=1, device_id=place((me + step) % count), device_id_type=MESH
        )
        return carry

    lax.fori_loop(1, count, greet, 0)

    def swap(n, carry):
        for source, target in ((blocks, block_t), (inverse, inverse_t)):
            rows = source[n].astype(jnp.float32)
            for t in range(tiles):
                target[t, pl.ds(n, NODES, stride=NODES), :] = rows[:, t * 128 : (t + 1) * 128]
        return carry

    lax.fori_loop(0, NODES, swap, 0)

    def apply_blocks(source, emit):
        for t in range(tiles):
            def outer(pair, carry):
                base = pl.multiple_of(pair * 16, 16)

                def inner(step, total):
                    total = list(total)
                    for u in range(4):
                        k = step * 4 + u
                        low = source[t, pl.ds(k * NODES + base, 8), :]
                        high = source[t, pl.ds(k * NODES + base + 8, 8), :]
                        for c in range(COMPS):
                            value = bcast[t, pl.ds(c * NODES + k, 8, stride=0), :]
                            total[2 * c] = total[2 * c] + low * value
                            total[2 * c + 1] = total[2 * c + 1] + high * value
                    return tuple(total)

                zero = jnp.zeros((8, 128), jnp.float32)
                total = lax.fori_loop(0, NODES // 4, inner, (zero,) * (2 * COMPS))
                for c in range(COMPS):
                    for h in range(2):
                        rows = pl.ds(c * NODES + base + 8 * h, 8)
                        emit(rows, slice(t * 128, (t + 1) * 128), total[2 * c + h])
                return carry

            lax.fori_loop(0, NODES // 16, outer, 0)

    def spread(value):
        rounded = value.astype(jnp.bfloat16).astype(jnp.float32)
        for t in range(tiles):
            bcast[t] = rounded[:, t * 128 : (t + 1) * 128]

    def store(target):
        def emit(rows, lanes, value):
            target[rows, lanes] = value
        return emit

    spread(rhs[...])
    apply_blocks(inverse_t, store(state))

    jac_t = jac[...].astype(jnp.bfloat16)
    spread_jac = dot(jac_t, comp_col[...]).astype(jnp.bfloat16)

    def tables(f, carry):
        rows = pl.ds(pl.multiple_of(f * SIDE, SIDE), SIDE)
        value = dot(row_comp[rows, :], spread_jac) * dot(row_node[rows, :], node_col[...])
        trace_t[rows, :] = (PENALTY * value).astype(jnp.bfloat16)
        return carry

    lax.fori_loop(0, FACES, tables, 0)

    def lifts(i, carry):
        rows = pl.ds(pl.multiple_of(i * 208, 208), 208)
        value = dot(col_comp[rows, :], comp_row[...]) * dot(col_node[rows, :], node_row[...])
        lift_t[rows, :] = value.astype(jnp.bfloat16)
        return carry

    lax.fori_loop(0, FLAT // 208, lifts, 0)

    def column(row):
        element = (row * 43691) >> 18
        return jnp.where(row < own, (row - element * FACES) * elements + element, row)

    def one_hot(rows, wanted):
        index = lax.broadcasted_iota(jnp.int32, (rows, wanted.shape[1]), 0)
        return jnp.where(index == wanted, 1.0, 0.0).astype(jnp.bfloat16)

    for k in range(ROUNDS):
        pick_send[:, k * 128 : (k + 1) * 128] = one_hot(own, column(send_face[k : k + 1, :]))
    for f in range(FACES):
        wanted = column(face_src[f : f + 1, :])
        pick_local[f] = one_hot(own, wanted)
        pick_remote[f] = one_hot(far, wanted - own)
    route_row = (route[...] // MOST) * 8 + route[...] % MOST
    to_bucket = (
        lax.broadcasted_iota(jnp.int32, (count * 8, elements), 0) == route_row
    ).astype(jnp.float32)

    pl.semaphore_wait(barrier, count - 1)

    def operate(number):
        half_field[...] = state[...].astype(jnp.bfloat16)

        def traces(f, carry):
            rows = pl.ds(pl.multiple_of(f * SIDE, SIDE), SIDE)
            value = dot(trace_t[rows, :], half_field[...])
            trace[rows, :] = value
            table[:, pl.ds(pl.multiple_of(f * elements, 128), elements)] = value.astype(
                jnp.bfloat16
            )
            return carry

        lax.fori_loop(0, FACES, traces, 0)
        copies = []
        for k in range(ROUNDS):
            sending[k] = dot(table[:, :own], pick_send[:, k * 128 : (k + 1) * 128])
            copy = pltpu.make_async_remote_copy(
                src_ref=sending.at[k],
                dst_ref=arriving.at[number, k],
                send_sem=send_sem.at[number, k],
                recv_sem=recv_sem.at[number, k],
                device_id=place(partner(k)),
                device_id_type=MESH,
            )
            copy.start()
            copies.append(copy)
        spread(state[...])
        apply_blocks(block_t, store(work))

        def near(f, carry):
            rows = pl.ds(pl.multiple_of(f * SIDE, SIDE), SIDE)
            beside[rows, :] = trace[rows, :] - dot(table[:, :own], pick_local[f])
            return carry

        lax.fori_loop(0, FACES, near, 0)
        for k in range(ROUNDS):
            copies[k].wait()
            table[:, own + k * 128 : own + (k + 1) * 128] = arriving[number, k].astype(
                jnp.bfloat16
            )

        def beyond(f, carry):
            rows = pl.ds(pl.multiple_of(f * SIDE, SIDE), SIDE)
            value = beside[rows, :] - dot(table[:, own:], pick_remote[f])
            jump[rows, :] = value.astype(jnp.bfloat16)
            return carry

        lax.fori_loop(0, FACES, beyond, 0)

        def lift(i, carry):
            rows = pl.ds(pl.multiple_of(i * 208, 208), 208)
            lifted[rows, :] = rhs[rows, :] - work[rows, :] - dot(lift_t[rows, :], jump[...])
            return carry

        lax.fori_loop(0, FLAT // 208, lift, 0)

    def sweep(number, target):
        operate(number)
        spread(lifted[...])

        def emit(rows, lanes, value):
            target[rows, lanes] = state[rows, lanes] + value

        apply_blocks(inverse_t, emit)

    def exchange(source, target, sent, got):
        def copy_of(step):
            other = (me + step) % count
            return pltpu.make_async_remote_copy(
                src_ref=source.at[other],
                dst_ref=target.at[me],
                send_sem=sent.at[step],
                recv_sem=got.at[step],
                device_id=place(other),
                device_id_type=MESH,
            )

        def begin(step, carry):
            copy_of(step).start()
            return carry

        def finish(step, carry):
            copy_of(step).wait()
            return carry

        lax.fori_loop(1, count, begin, 0)
        target[me] = source[me]
        lax.fori_loop(1, count, finish, 0)

    sweep(0, state)
    operate(1)
    partial = dot_exact(restrict_t[...], lifted[...])
    bucket[...] = dot_exact(to_bucket, partial, ((1,), (1,))).reshape(count, 8, 128)
    exchange(bucket, incoming, give_sem, take_sem)
    owned = cblock.shape[0]
    gather_in = (
        lax.broadcasted_iota(jnp.int32, (owned, count * 8), 0) == agg_row[...]
    ).astype(jnp.float32)
    coarse_rhs = dot_exact(gather_in, incoming[...].reshape(count * 8, 128))
    inv_wide = dot_exact(cinv[...], coef[...])
    block_wide = dot_exact(cblock[...], coef[...])

    def modal(wide, value):
        product = wide * dot_exact(value, pick[...])
        return (
            product[:, :128] + product[:, 128:256] + product[:, 256:384] + product[:, 384:]
        )

    first = modal(inv_wide, coarse_rhs)
    solved = first + modal(inv_wide, coarse_rhs - modal(block_wide, first))
    gather_out = (
        lax.broadcasted_iota(jnp.int32, (count * 8, owned), 1) == agg_col[...]
    ).astype(jnp.float32)
    reply[...] = dot_exact(gather_out, solved).reshape(count, 8, 128)
    exchange(reply, answer, back_sem, home_sem)
    correction = dot_exact(answer[...].reshape(count * 8, 128), to_bucket, ((0,), (0,)))
    state[...] = state[...] + dot_exact(basis_t[...], correction)
    sweep(2, state)
    sweep(3, out)


def local(
    rhs,
    elem_block,
    block_inv,
    flux_jac,
    face_src,
    send_face,
    elem_route,
    agg_local,
    coarse_block,
    coarse_inv,
):
    elements = rhs.shape[0]
    count = lax.axis_size(("dom", "sub"))
    subs = lax.axis_size("sub")
    owned = coarse_block.shape[0]
    tiles = elements // 128
    own = FACES * elements
    far = ROUNDS * 128
    padded = jnp.pad(agg_local, ((0, 0), (0, 8 - MOST)), constant_values=-1)
    f32, half = jnp.float32, jnp.bfloat16
    dma = pltpu.SemaphoreType.DMA
    result = pl.pallas_call(
        functools.partial(kernel, count, subs),
        out_shape=jax.ShapeDtypeStruct((FLAT, elements), f32),
        in_specs=[pl.BlockSpec(memory_space=pltpu.VMEM)] * 23,
        out_specs=pl.BlockSpec(memory_space=pltpu.VMEM),
        scratch_shapes=[
            pltpu.VMEM((tiles, NODES * NODES, 128), f32),
            pltpu.VMEM((tiles, NODES * NODES, 128), f32),
            pltpu.VMEM((tiles, FLAT, 128), f32),
            pltpu.VMEM((FLAT, TRACE), half),
            pltpu.VMEM((TRACE, FLAT), half),
            pltpu.VMEM((FACES, own, elements), half),
            pltpu.VMEM((FACES, far, elements), half),
            pltpu.VMEM((own, far), half),
            pltpu.VMEM((FLAT, elements), half),
            pltpu.VMEM((FLAT, elements), f32),
            pltpu.VMEM((FLAT, elements), f32),
            pltpu.VMEM((FLAT, elements), f32),
            pltpu.VMEM((TRACE, elements), f32),
            pltpu.VMEM((TRACE, elements), f32),
            pltpu.VMEM((SIDE, own + far), half),
            pltpu.VMEM((TRACE, elements), half),
            pltpu.VMEM((ROUNDS, SIDE, 128), f32),
            pltpu.VMEM((4, ROUNDS, SIDE, 128), f32),
            pltpu.VMEM((count, 8, 128), f32),
            pltpu.VMEM((count, 8, 128), f32),
            pltpu.VMEM((count, 8, 128), f32),
            pltpu.VMEM((count, 8, 128), f32),
            dma((4, ROUNDS)),
            dma((4, ROUNDS)),
            dma((count,)),
            dma((count,)),
            dma((count,)),
            dma((count,)),
        ],
        compiler_params=pltpu.CompilerParams(
            collective_id=0, has_side_effects=True, vmem_limit_bytes=58 * 2**20
        ),
    )(
        rhs.T,
        elem_block.transpose(1, 2, 0),
        block_inv.transpose(1, 2, 0),
        jnp.pad(flux_jac.T, ((0, 3), (0, 3))),
        face_src.T,
        send_face,
        elem_route.reshape(1, elements),
        padded.reshape(count * 8, 1),
        padded.reshape(1, count * 8),
        coarse_block.reshape(owned, MODES * MODES),
        coarse_inv.reshape(owned, MODES * MODES),
        *const_tables(),
    )
    return result.T


def solution(mesh):
    return jax.shard_map(
        local,
        mesh=mesh,
        in_specs=(
            P(("dom", "sub"), None),
            P(("dom", "sub"), None, None),
            P(("dom", "sub"), None, None),
            P(),
            P(("dom", "sub"), None),
            P(("dom", "sub"), None),
            P(("dom", "sub")),
            P(("dom", "sub"), None),
            P(("dom", "sub"), None, None),
            P(("dom", "sub"), None, None),
        ),
        out_specs=P(("dom", "sub"), None),
        check_vma=False,
    )
```

```python
import functools
import math

import jax
import jax.numpy as jnp
import numpy as np
from jax import lax
from jax.experimental import pallas as pl
from jax.experimental.pallas import tpu as pltpu
from jax.sharding import PartitionSpec as P

COMPS = 13
NODES = 64
FACES = 6
FACE_NODES = 16
MODES = 4
ROUNDS = 5
MOST = 2
FLAT = COMPS * NODES
PITCH = NODES + 8
SIDE = COMPS * FACE_NODES
TRACE = FACES * SIDE

HIGHEST = lax.Precision.HIGHEST
PENALTY = 0.5
MESH = pl.DeviceIdType.MESH


def node_tables():
    points = np.array([-1.0, -1.0 / math.sqrt(5.0), 1.0 / math.sqrt(5.0), 1.0])
    weights = np.array([1.0, 5.0, 5.0, 1.0]) / 6.0
    grid_i, grid_j, grid_k = np.meshgrid(points, points, points, indexing="ij")
    weight_grid = weights[:, None, None] * weights[None, :, None] * weights[None, None, :] / 8.0
    basis = np.stack([np.ones(64), grid_i.reshape(-1), grid_j.reshape(-1), grid_k.reshape(-1)])
    restrict = basis * weight_grid.reshape(-1)[None, :]
    number = np.arange(64).reshape(4, 4, 4)
    sides = [number[0], number[3], number[:, 0], number[:, 3], number[:, :, 0], number[:, :, 3]]
    face_index = np.stack([side.reshape(-1) for side in sides])
    return basis, restrict, face_index


def const_tables():
    basis, restrict, face_index = node_tables()
    eye = np.eye(COMPS)
    row_comp = np.tile(np.repeat(eye, FACE_NODES, axis=0), (FACES, 1))
    row_comp = np.pad(row_comp, ((0, 0), (0, 3)))
    col_comp = np.pad(np.repeat(eye, NODES, axis=0), ((0, 0), (0, 3)))
    node = np.eye(NODES)[face_index]
    row_node = np.broadcast_to(node[:, None], (FACES, COMPS, FACE_NODES, NODES)).reshape(TRACE, NODES)
    col_node = np.tile(np.eye(NODES), (COMPS, 1))
    restrict_t = np.zeros((128, FLAT))
    restrict_t[: COMPS * MODES] = np.kron(eye, restrict)
    basis_t = np.zeros((FLAT, 128))
    basis_t[:, : COMPS * MODES] = np.kron(eye, basis.T)
    pick = np.zeros((128, MODES * 128))
    coef = np.zeros((16, MODES * 128))
    for k in range(MODES):
        for c in range(COMPS):
            for m in range(MODES):
                pick[c * MODES + k, k * 128 + c * MODES + m] = 1.0
                coef[m * MODES + k, k * 128 + c * MODES + m] = 1.0
    half = jnp.bfloat16
    return (
        jnp.asarray(row_comp, half),
        jnp.asarray(row_node, half),
        jnp.asarray(col_comp.T, half),
        jnp.asarray(col_node.T, half),
        jnp.asarray(col_comp, half),
        jnp.asarray(col_node, half),
        jnp.asarray(row_comp.T, half),
        jnp.asarray(row_node.T, half),
        jnp.asarray(restrict_t, jnp.float32),
        jnp.asarray(basis_t, jnp.float32),
        jnp.asarray(pick, jnp.float32),
        jnp.asarray(coef, jnp.float32),
    )


def dot(a, b):
    return jnp.dot(a, b, preferred_element_type=jnp.float32)


def dot_exact(a, b, dims=((1,), (0,))):
    return lax.dot_general(
        a, b, (dims, ((), ())), precision=HIGHEST, preferred_element_type=jnp.float32
    )


def kernel(
    count, subs,
    rhs, blocks, inverse, jac, face_src, send_face, route, agg_local, cblock, cinv,
    row_comp, row_node, comp_col, node_col, col_comp, col_node, comp_row, node_row,
    restrict_t, basis_t, pick, coef,
    out,
    block_t, inverse_t, bcast, lift_t, trace_t, pick_local, pick_remote, pick_send,
    half_field, state, work, lifted, trace, beside, table, jump, sending, arriving,
    bucket, incoming, reply, answer, jac_pad, flat_block, flat_inv,
    send_sem, recv_sem, give_sem, take_sem, back_sem, home_sem,
):
    elements = rhs.shape[1]
    tiles = elements // 128
    own = FACES * elements
    far = ROUNDS * 128
    me = lax.axis_index("dom") * subs + lax.axis_index("sub")

    def place(flat):
        return (flat // subs, flat % subs)

    def partner(k):
        bit = 1 << k
        return me + bit * (1 - 2 * ((me // bit) % 2))

    barrier = pltpu.get_barrier_semaphore()

    def greet(step, carry):
        pl.semaphore_signal(
            barrier, inc=1, device_id=place((me + step) % count), device_id_type=MESH
        )
        return carry

    lax.fori_loop(1, count, greet, 0)

    def swap(n, carry):
        for source, target in ((blocks, block_t), (inverse, inverse_t)):
            rows = source[n].astype(jnp.float32)
            for t in range(tiles):
                target[t, pl.ds(n, NODES, stride=PITCH), :] = rows[:, t * 128 : (t + 1) * 128]
        return carry

    lax.fori_loop(0, NODES, swap, 0)

    def apply_blocks(source, emit):
        for t in range(tiles):
            def outer(quad, carry):
                base = pl.multiple_of(quad * 32, 32)
                for comps in (range(0, 7), range(7, COMPS)):
                    def inner(step, total):
                        total = list(total)
                        for u in range(4):
                            k = step * 4 + u
                            parts = [
                                source[t, pl.ds(k * PITCH + base + 8 * h, 8), :] for h in range(4)
                            ]
                            for i, c in enumerate(comps):
                                value = bcast[t, pl.ds(c * NODES + k, 8, stride=0), :]
                                for h in range(4):
                                    total[4 * i + h] = total[4 * i + h] + parts[h] * value
                        return tuple(total)

                    zero = jnp.zeros((8, 128), jnp.float32)
                    total = lax.fori_loop(0, NODES // 4, inner, (zero,) * (4 * len(comps)))
                    for i, c in enumerate(comps):
                        for h in range(4):
                            rows = pl.ds(c * NODES + base + 8 * h, 8)
                            emit(rows, slice(t * 128, (t + 1) * 128), total[4 * i + h])
                return carry

            lax.fori_loop(0, NODES // 32, outer, 0)

    def spread(value):
        rounded = value.astype(jnp.bfloat16).astype(jnp.float32)
        for t in range(tiles):
            bcast[t] = rounded[:, t * 128 : (t + 1) * 128]

    def store(target):
        def emit(rows, lanes, value):
            target[rows, lanes] = value
        return emit

    spread(rhs[...])
    apply_blocks(inverse_t, store(state))

    jac_pad[...] = jnp.zeros_like(jac_pad)
    jac_pad[:COMPS, :COMPS] = jac[...]
    spread_jac = lax.dot_general(
        jac_pad[...].astype(jnp.bfloat16),
        comp_col[...],
        (((0,), (0,)), ((), ())),
        preferred_element_type=jnp.float32,
    )[:16].astype(jnp.bfloat16)
    for m in range(MODES):
        flat_block[m * MODES : (m + 1) * MODES, :] = cblock[m]
        flat_inv[m * MODES : (m + 1) * MODES, :] = cinv[m]
    inv_wide = dot_exact(flat_inv[...], coef[...], ((0,), (0,)))
    block_wide = dot_exact(flat_block[...], coef[...], ((0,), (0,)))

    def tables(f, carry):
        rows = pl.ds(pl.multiple_of(f * SIDE, SIDE), SIDE)
        value = dot(row_comp[rows, :], spread_jac) * dot(row_node[rows, :], node_col[...])
        trace_t[rows, :] = (PENALTY * value).astype(jnp.bfloat16)
        return carry

    lax.fori_loop(0, FACES, tables, 0)

    def lifts(i, carry):
        rows = pl.ds(pl.multiple_of(i * 208, 208), 208)
        value = dot(col_comp[rows, :], comp_row[...]) * dot(col_node[rows, :], node_row[...])
        lift_t[rows, :] = value.astype(jnp.bfloat16)
        return carry

    lax.fori_loop(0, FLAT // 208, lifts, 0)

    def column(row):
        element = (row * 43691) >> 18
        return jnp.where(row < own, (row - element * FACES) * elements + element, row)

    def one_hot(rows, wanted):
        index = lax.broadcasted_iota(jnp.int32, (rows, wanted.shape[1]), 0)
        return jnp.where(index == wanted, 1.0, 0.0).astype(jnp.bfloat16)

    for k in range(ROUNDS):
        pick_send[:, k * 128 : (k + 1) * 128] = one_hot(own, column(send_face[k : k + 1, :]))
    for f in range(FACES):
        wanted = column(face_src[f : f + 1, :])
        pick_local[f] = one_hot(own, wanted)
        pick_remote[f] = one_hot(far, wanted - own)
    route_row = (route[...] // MOST) * 8 + route[...] % MOST
    to_bucket = (
        lax.broadcasted_iota(jnp.int32, (count * 8, elements), 0) == route_row
    ).astype(jnp.float32)

    pl.semaphore_wait(barrier, count - 1)

    def operate(number):
        half_field[...] = state[...].astype(jnp.bfloat16)

        def traces(third, carry):
            rows = pl.ds(pl.multiple_of(third * 2 * SIDE, 2 * SIDE), 2 * SIDE)
            value = dot(trace_t[rows, :], half_field[...])
            trace[rows, :] = value
            column_pair = pl.ds(pl.multiple_of(third * 2 * elements, 128), elements)
            table[:, column_pair] = value[:SIDE].astype(jnp.bfloat16)
            column_pair = pl.ds(pl.multiple_of((third * 2 + 1) * elements, 128), elements)
            table[:, column_pair] = value[SIDE:].astype(jnp.bfloat16)
            return carry

        lax.fori_loop(0, FACES // 2, traces, 0)
        outgoing = dot(table[:, :own], pick_send[...])
        copies = []
        for k in range(ROUNDS):
            sending[k] = outgoing[:, k * 128 : (k + 1) * 128]
            copy = pltpu.make_async_remote_copy(
                src_ref=sending.at[k],
                dst_ref=arriving.at[number, k],
                send_sem=send_sem.at[number, k],
                recv_sem=recv_sem.at[number, k],
                device_id=place(partner(k)),
                device_id_type=MESH,
            )
            copy.start()
            copies.append(copy)
        spread(state[...])
        apply_blocks(block_t, store(work))

        def near(f, carry):
            rows = pl.ds(pl.multiple_of(f * SIDE, SIDE), SIDE)
            beside[rows, :] = trace[rows, :] - dot(table[:, :own], pick_local[f])
            return carry

        lax.fori_loop(0, FACES, near, 0)
        for k in range(ROUNDS):
            copies[k].wait()
            table[:, own + k * 128 : own + (k + 1) * 128] = arriving[number, k].astype(
                jnp.bfloat16
            )

        def beyond(f, carry):
            rows = pl.ds(pl.multiple_of(f * SIDE, SIDE), SIDE)
            value = beside[rows, :] - dot(table[:, own:], pick_remote[f])
            jump[rows, :] = value.astype(jnp.bfloat16)
            return carry

        lax.fori_loop(0, FACES, beyond, 0)

        def lift(i, carry):
            rows = pl.ds(pl.multiple_of(i * 416, 416), 416)
            lifted[rows, :] = rhs[rows, :] - work[rows, :] - dot(lift_t[rows, :], jump[...])
            return carry

        lax.fori_loop(0, FLAT // 416, lift, 0)

    def sweep(number, target):
        operate(number)
        spread(lifted[...])

        def emit(rows, lanes, value):
            target[rows, lanes] = state[rows, lanes] + value

        apply_blocks(inverse_t, emit)

    def exchange(source, target, sent, got):
        def copy_of(step):
            other = (me + step) % count
            return pltpu.make_async_remote_copy(
                src_ref=source.at[other],
                dst_ref=target.at[me],
                send_sem=sent.at[step],
                recv_sem=got.at[step],
                device_id=place(other),
                device_id_type=MESH,
            )

        def begin(step, carry):
            copy_of(step).start()
            return carry

        def finish(step, carry):
            copy_of(step).wait()
            return carry

        lax.fori_loop(1, count, begin, 0)
        target[me] = source[me]
        lax.fori_loop(1, count, finish, 0)

    sweep(0, state)
    operate(1)
    partial = dot_exact(restrict_t[...], lifted[...])
    bucket[...] = dot_exact(to_bucket, partial, ((1,), (1,))).reshape(count, 8, 128)
    exchange(bucket, incoming, give_sem, take_sem)
    owned = cblock.shape[2]
    members = [
        (
            lax.broadcasted_iota(jnp.int32, (owned, count), 0) == agg_local[s : s + 1, :]
        ).astype(jnp.float32)
        for s in range(MOST)
    ]
    coarse_rhs = sum(dot_exact(members[s], incoming[:, s, :]) for s in range(MOST))

    def modal(wide, value):
        product = wide * dot_exact(value, pick[...])
        return (
            product[:, :128] + product[:, 128:256] + product[:, 256:384] + product[:, 384:]
        )

    first = modal(inv_wide, coarse_rhs)
    solved = first + modal(inv_wide, coarse_rhs - modal(block_wide, first))
    reply[...] = jnp.zeros_like(reply)
    for s in range(MOST):
        reply[:, s, :] = dot_exact(members[s], solved, ((0,), (0,)))
    exchange(reply, answer, back_sem, home_sem)
    correction = dot_exact(answer[...].reshape(count * 8, 128), to_bucket, ((0,), (0,)))
    state[...] = state[...] + dot_exact(basis_t[...], correction)
    def last_sweeps(number, carry):
        sweep(number, state)
        return carry

    lax.fori_loop(2, 4, last_sweeps, 0)
    out[...] = state[...]


def local(
    rhs,
    elem_block,
    block_inv,
    flux_jac,
    face_src,
    send_face,
    elem_route,
    agg_local,
    coarse_block,
    coarse_inv,
):
    elements = rhs.shape[0]
    count = lax.axis_size(("dom", "sub"))
    subs = lax.axis_size("sub")
    owned = coarse_block.shape[0]
    tiles = elements // 128
    own = FACES * elements
    far = ROUNDS * 128
    f32, half = jnp.float32, jnp.bfloat16
    dma = pltpu.SemaphoreType.DMA
    result = pl.pallas_call(
        functools.partial(kernel, count, subs),
        out_shape=jax.ShapeDtypeStruct((FLAT, elements), f32),
        in_specs=[pl.BlockSpec(memory_space=pltpu.VMEM)] * 22,
        out_specs=pl.BlockSpec(memory_space=pltpu.VMEM),
        scratch_shapes=[
            pltpu.VMEM((tiles, NODES * PITCH, 128), f32),
            pltpu.VMEM((tiles, NODES * PITCH, 128), f32),
            pltpu.VMEM((tiles, FLAT, 128), f32),
            pltpu.VMEM((FLAT, TRACE), half),
            pltpu.VMEM((TRACE, FLAT), half),
            pltpu.VMEM((FACES, own, elements), half),
            pltpu.VMEM((FACES, far, elements), half),
            pltpu.VMEM((own, far), half),
            pltpu.VMEM((FLAT, elements), half),
            pltpu.VMEM((FLAT, elements), f32),
            pltpu.VMEM((FLAT, elements), f32),
            pltpu.VMEM((FLAT, elements), f32),
            pltpu.VMEM((TRACE, elements), f32),
            pltpu.VMEM((TRACE, elements), f32),
            pltpu.VMEM((SIDE, own + far), half),
            pltpu.VMEM((TRACE, elements), half),
            pltpu.VMEM((ROUNDS, SIDE, 128), f32),
            pltpu.VMEM((4, ROUNDS, SIDE, 128), f32),
            pltpu.VMEM((count, 8, 128), f32),
            pltpu.VMEM((count, 8, 128), f32),
            pltpu.VMEM((count, 8, 128), f32),
            pltpu.VMEM((count, 8, 128), f32),
            pltpu.VMEM((16, 128), f32),
            pltpu.VMEM((MODES * MODES, owned), f32),
            pltpu.VMEM((MODES * MODES, owned), f32),
            dma((4, ROUNDS)),
            dma((4, ROUNDS)),
            dma((count,)),
            dma((count,)),
            dma((count,)),
            dma((count,)),
        ],
        compiler_params=pltpu.CompilerParams(
            collective_id=0, has_side_effects=True, vmem_limit_bytes=58 * 2**20
        ),
    )(
        rhs.T,
        elem_block.transpose(1, 2, 0),
        block_inv.transpose(1, 2, 0),
        flux_jac,
        face_src.T,
        send_face,
        elem_route.reshape(1, elements),
        agg_local.T,
        coarse_block.transpose(1, 2, 0),
        coarse_inv.transpose(1, 2, 0),
        *const_tables(),
    )
    return result.T


def solution(mesh):
    return jax.shard_map(
        local,
        mesh=mesh,
        in_specs=(
            P(("dom", "sub"), None),
            P(("dom", "sub"), None, None),
            P(("dom", "sub"), None, None),
            P(),
            P(("dom", "sub"), None),
            P(("dom", "sub"), None),
            P(("dom", "sub")),
            P(("dom", "sub"), None),
            P(("dom", "sub"), None, None),
            P(("dom", "sub"), None, None),
        ),
        out_specs=P(("dom", "sub"), None),
        check_vma=False,
    )
```
